128 devices in a mesh: grp: 8 (over z, core), mem: 16 (over y, x).
Axes of the slice: x: 4, y: 4, z: 4, core: 2. Of those that a mesh axis runs over, the one named last changes fastest.
Arguments:
- forcing: float32 [3, 1024, 4096], P(None, ('grp', 'mem')), may hold values from -6 to 6
- viscosity: float32 [1024, 4096], P(('grp', 'mem')), may hold values from 0.1 to 10
- refinement: int32 [1024], P(('grp', 'mem')), may hold values from 0 to 1
- face_owner: int32 [4096, 1], P(('grp', 'mem')), may hold values from 0 to 15; in each aligned block of 32 rows (0 to 31, 32 to 63, ...) at most 4 rows name the same one
- face_block: int32 [1024, 4], P(('grp', 'mem')), may hold values from 0 to 7
- plane_block: int32 [1024, 2], P(('grp', 'mem')), may hold values from 0 to 7
- hanging: int32 [1024, 6], P(('grp', 'mem')), may hold values 0 or 1
- coarse_solver: float32 [8, 384, 384], P('grp', 'mem'), may hold values from -0.3125 to 0.3125
Outputs:
- velocity: float32 [3, 1024, 4096], P(None, ('grp', 'mem'))
- residual: float32 [3, 1024, 4096], P(None, ('grp', 'mem'))
The draws below stay inside these ranges and needn't reach their ends.
Inputs may be any that keep to these rules, and one draw needn't show every extreme that they name: `face_owner`: among the 32 rows of one device no member appears more than 4 times, and some member appears exactly 4 times.
All inputs are finite; a program needn't handle non-finite values. No bound on the sum of `hanging` on one device may be relied on, other than what follows from the above.
Results may differ from the reference program's by a relative error of at most 0.0001.
Values sent between devices are 32-bit elements; how exact they have to be, the bound alone decides.
A program may use at most 64 MiB of HBM per device.

```python
import math
import jax
import jax.numpy as jnp
import numpy as np
from jax import lax

EDGE = 16
B_DEV = 8
DEG = 3
CELLS = 4096
FACE = 256
BLOCKS = 1024
CAP = 4
NC = 384
N_GRP = 8
N_MEM = 16


def place_ends(values, rng, smallest, top_value):
    place = [jax.random.randint(jax.random.fold_in(rng, axis), (), 0, length) for axis, length in enumerate(values.shape)]
    longest = values.shape.index(max(values.shape))
    next_to = place[:longest] + [(place[longest] + 1) % values.shape[longest]] + place[longest + 1:]
    return values.at[tuple(place)].set(smallest).at[tuple(next_to)].set(top_value)


def level_of(rng, dims, pieces, smallest, largest):
    loudness, own = 1.0, jax.random.fold_in(rng, 6)
    for dim, parts in pieces:
        steps = jnp.exp(jax.random.uniform(jax.random.fold_in(own, dim), (parts,), jnp.float32, smallest / len(pieces), largest / len(pieces)))
        loudness = loudness * jnp.repeat(steps, dims[dim] // parts).reshape([-1 if axis == dim else 1 for axis in range(len(dims))])
    return loudness


def shared_out(stream_key, own, number, rows, amount, top, most, slope):
    order = jax.random.permutation(stream_key, amount)
    crowded, usual = load_shares(amount, rows * top, most, slope, True), load_shares(amount, rows * top, most, slope, False)
    places = jnp.arange(amount)

    def named(lengths, turn):
        used = int((lengths > 0).sum())
        fixed = max(1, used // 4)
        moved = fixed + (places - fixed + turn * (used - fixed)) % max(1, amount - fixed)
        return jnp.zeros((amount,), jnp.int32).at[order[jnp.where(places < fixed, places, moved)]].set(jnp.asarray(lengths, jnp.int32))

    lengths = jnp.where(number % 4 == 0, named(crowded, number // 4), named(usual, number - number // 4 - 1))
    mixed = jax.random.permutation(jax.random.fold_in(own, 3), amount)
    donor, sink = mixed[0:amount // 2 * 2:2], mixed[1:amount // 2 * 2:2]
    margin = jnp.minimum(lengths[donor] - 1, most - lengths[sink]) // 2
    margin = jnp.where((donor == order[0]) | (sink == order[0]) | (lengths[sink] == 0), 0, jnp.maximum(margin, 0))
    moved = jax.random.randint(jax.random.fold_in(own, 4), (amount // 2,), 0, 1 << 20) % (margin + 1)
    lengths = lengths.at[donor].add(-moved).at[sink].add(moved)
    members = jnp.searchsorted(jnp.cumsum(lengths), jnp.arange(rows * top), side="right").astype(jnp.int32)
    grid = members.reshape(top, rows).T
    grid = grid[jax.random.permutation(jax.random.fold_in(own, 1), rows)]
    turn = jax.random.randint(jax.random.fold_in(own, 2), (rows, 1), 0, top)
    return jnp.take_along_axis(grid, (jnp.arange(top)[None, :] + turn) % top, axis=1)


def load_shares(amount, total, reach, skew, full):
    weights = [(1 << 20) // math.isqrt(rank ** skew) + 1 for rank in range(1, amount + 1)]
    largest = reach if full else min(reach, max(-(-total // amount), total * weights[0] // sum(weights)))
    least = 1 if total - largest >= amount - 1 else 0
    holding, surplus = [largest] + [least] * (amount - 1), total - largest - least * (amount - 1)
    while surplus > 0:
        candidates = [i for i in range(1, amount) if holding[i] < largest] or [i for i in range(1, amount) if holding[i] < reach]
        pool, remaining = sum([weights[i] for i in candidates]), surplus
        for i in candidates:
            addition = min(reach - holding[i], max(1, remaining * weights[i] // pool), surplus)
            holding[i] = holding[i] + addition
            surplus = surplus - addition
    return np.array(holding)


def centred(key, shape, deviation, reach, shards=(), kind=jnp.bfloat16):
    values = deviation * jax.random.normal(key, shape, jnp.float32)
    if shards:
        values = values * level_of(key, shape, shards, -0.22, 0.18)
    return jnp.clip(values, -reach, reach).astype(kind)


def setup_inputs(seed: int = 0) -> dict:
    seeds = jax.random.split(jax.random.key(seed), 9)
    forcing = centred(seeds[0], (3, BLOCKS, CELLS), 1.0, 6.0, ((1, 128),), jnp.float32)
    viscosity = jnp.clip(jnp.exp(math.log(10.0) - 4.6051702 * jax.random.uniform(seeds[1], (BLOCKS, CELLS), jnp.float32) ** level_of(seeds[1], (BLOCKS, CELLS), ((0, 128),), -0.2, 0.2)), 0.1, 10.0)
    refinement = place_ends(jax.random.randint(seeds[2], (BLOCKS,), 0, 2), jax.random.fold_in(seeds[2], 1), 0, 1).astype(jnp.int32)
    face_owner_keys = jax.random.split(jax.random.fold_in(seeds[3], 1), (4 * BLOCKS) // (4 * B_DEV))
    face_owner_turns = jax.random.permutation(jax.random.fold_in(seeds[3], 3), (4 * BLOCKS) // (4 * B_DEV))
    face_owner = jax.vmap(lambda own, number: shared_out(jax.random.fold_in(seeds[3], 2), own, number, 4 * B_DEV, N_MEM, 1, CAP, 2))(face_owner_keys, face_owner_turns).reshape((4 * BLOCKS, 1))
    face_block = place_ends(jax.random.randint(seeds[4], (BLOCKS, 4), 0, B_DEV), jax.random.fold_in(seeds[4], 1), 0, B_DEV - 1).astype(jnp.int32)
    plane_block = place_ends(jax.random.randint(seeds[5], (BLOCKS, 2), 0, B_DEV), jax.random.fold_in(seeds[5], 1), 0, B_DEV - 1).astype(jnp.int32)
    hanging = place_ends((jax.random.randint(seeds[6], (BLOCKS, 6), 0, 4) < 1).astype(jnp.int32), jax.random.fold_in(seeds[6], 1), 0, 1)
    coarse_solver = centred(seeds[7], (N_GRP, NC, NC), NC ** -0.5, 0.3125, ((0, 8), (1, 16)), jnp.float32)
    return {"forcing": forcing, "viscosity": viscosity, "refinement": refinement, "face_owner": face_owner, "face_block": face_block, "plane_block": plane_block, "hanging": hanging, "coarse_solver": coarse_solver}


MASS_TERM = 1.0
LOWER_BOUND = 0.25
UPPER_BOUND = 2.0

def face_set(values):
    leading = values.shape[:-1]
    cube_view = values.reshape(leading + (EDGE, EDGE, EDGE))
    return [cube_view[..., 0].reshape(leading + (FACE,)), cube_view[..., EDGE - 1].reshape(leading + (FACE,)), cube_view[..., :, 0, :].reshape(leading + (FACE,)), cube_view[..., :, EDGE - 1, :].reshape(leading + (FACE,)), cube_view[..., 0, :, :].reshape(leading + (FACE,)), cube_view[..., EDGE - 1, :, :].reshape(leading + (FACE,))]

def coarsen(plane_vals):
    leading = plane_vals.shape[:-1]
    squares = plane_vals.reshape(leading + (EDGE // 2, 2, EDGE // 2, 2))
    average = lax.optimization_barrier(jnp.mean(squares, axis=(-3, -1), keepdims=True))
    return jnp.broadcast_to(average, squares.shape).reshape(leading + (FACE,))

def spread(plane_vals):
    leading = plane_vals.shape[:-1]
    shaped = plane_vals.reshape(leading + (EDGE, 1, EDGE))
    return jnp.broadcast_to(shaped, leading + (EDGE, EDGE, EDGE)).reshape(leading + (CELLS,))

def beside(values, ghosts):
    leading = values.shape[:-1]
    cell_index = jnp.arange(CELLS, dtype=jnp.int32)
    along_k = cell_index % EDGE
    along_j = cell_index // EDGE % EDGE
    zero_one = jnp.zeros(leading + (1,), jnp.float32)
    zero_row = jnp.zeros(leading + (EDGE,), jnp.float32)
    return [jnp.where(along_k == 0, jnp.repeat(ghosts[0], EDGE, axis=-1), jnp.concatenate([zero_one, values[..., :-1]], axis=-1)), jnp.where(along_k == EDGE - 1, jnp.repeat(ghosts[1], EDGE, axis=-1), jnp.concatenate([values[..., 1:], zero_one], axis=-1)), jnp.where(along_j == 0, spread(ghosts[2]), jnp.concatenate([zero_row, values[..., :-EDGE]], axis=-1)), jnp.where(along_j == EDGE - 1, spread(ghosts[3]), jnp.concatenate([values[..., EDGE:], zero_row], axis=-1)), jnp.concatenate([ghosts[4], values[..., :-FACE]], axis=-1), jnp.concatenate([values[..., FACE:], ghosts[5]], axis=-1)]

def reference(forcing, viscosity, refinement, face_owner, face_block, plane_block, hanging, coarse_solver):
    effective = viscosity * jnp.exp2(-refinement.astype(jnp.float32))[:, None]
    stride = N_MEM * B_DEV
    block_ids = jnp.arange(BLOCKS, dtype=jnp.int32)
    group_base = block_ids // stride * stride
    local_idx = block_ids % B_DEV
    owners = face_owner.reshape(BLOCKS, 4)
    sources = [group_base + owners[:, direction] * B_DEV + face_block[:, direction] for direction in range(4)]
    lower_src = jnp.clip(block_ids - stride - local_idx + plane_block[:, 0], 0, BLOCKS - 1).astype(jnp.int32)
    upper_src = jnp.clip(block_ids + stride - local_idx + plane_block[:, 1], 0, BLOCKS - 1).astype(jnp.int32)
    lower_valid = block_ids >= stride
    upper_valid = block_ids < BLOCKS - stride

    def ghost_set(stacked):
        planes = face_set(stacked)
        result = []
        for direction in range(4):
            result.append(planes[direction ^ 1][:, sources[direction]])
        result.append(jnp.where(lower_valid[None, :, None], planes[5][:, lower_src], 0.0))
        result.append(jnp.where(upper_valid[None, :, None], planes[4][:, upper_src], 0.0))
        return [jnp.where(hanging[:, direction][None, :, None] == 1, coarsen(result[direction]), result[direction]) for direction in range(6)]
    nearby_eff = beside(effective[None], ghost_set(effective[None]))
    weights = [0.5 * (effective + nearby_eff[direction][0]) for direction in range(6)]
    diagonal = MASS_TERM * effective
    for direction in range(6):
        diagonal = diagonal + weights[direction]

    def operate(values):
        nearby = beside(values, ghost_set(values))
        applied = diagonal * values
        for direction in range(6):
            applied = applied - weights[direction] * nearby[direction]
        return applied
    midpoint = 0.5 * (UPPER_BOUND + LOWER_BOUND)
    half_width = 0.5 * (UPPER_BOUND - LOWER_BOUND)
    sigma_ratio = midpoint / half_width

    def smooth(solution, residual):
        rho_now = 1.0 / sigma_ratio
        step_dir = residual / (diagonal * midpoint)
        for sweep_index in range(DEG):
            solution = solution + step_dir
            residual = residual - operate(step_dir)
            if sweep_index < DEG - 1:
                rho_next = 1.0 / (2.0 * sigma_ratio - rho_now)
                step_dir = rho_next * rho_now * step_dir + 2.0 * rho_next / half_width * (residual / diagonal)
                rho_now = rho_next
        return (solution, residual)
    solution, residual = smooth(jnp.zeros_like(forcing), forcing)
    coarse_vec = (lax.optimization_barrier(jnp.sum(residual, axis=-1)) / math.sqrt(CELLS)).T.reshape(N_GRP, NC)
    correction = jnp.einsum('gij,gj->gi', coarse_solver, coarse_vec, precision=lax.Precision.HIGHEST)
    lifted = jnp.broadcast_to(correction.reshape(BLOCKS, 3).T[:, :, None], forcing.shape)
    solution = solution + lifted
    residual = residual - operate(lifted)
    solution, residual = smooth(solution, residual)
    return (solution, residual)
```

```python
import functools
import math

import jax
import jax.numpy as jnp
from jax import lax
from jax.experimental import pallas as pl
from jax.experimental.pallas import tpu as pltpu
from jax.sharding import PartitionSpec as P

EDGE = 16
DEG = 3
CELLS = 4096
CAP = 4
B = 8
LANES = 128
ROWS = 8
NC = 384

MASS_TERM = 1.0
LOWER_BOUND = 0.25
UPPER_BOUND = 2.0
MIDPOINT = 0.5 * (UPPER_BOUND + LOWER_BOUND)
HALF_WIDTH = 0.5 * (UPPER_BOUND - LOWER_BOUND)
SIGMA = MIDPOINT / HALF_WIDTH

MESH = pl.DeviceIdType.MESH
F32 = jnp.float32


def plan_kernel(members, owner_ref, block_ref, want_ref, pos_ref, count):
    sub = lax.broadcasted_iota(jnp.int32, (members, 1, LANES), 0)
    lane = lax.broadcasted_iota(jnp.int32, (members, 1, LANES), 2)
    for m in range(members):
        count[m] = 0
    want = jnp.zeros((members, 1, LANES), jnp.int32)
    for row in range(4 * B):
        b, d = row // 4, row % 4
        owner = owner_ref[row, 0]
        slot = count[owner]
        count[owner] = slot + 1
        pos_ref[row] = owner * CAP + slot
        tile = (d ^ 1) * B + block_ref[b, d]
        want = jnp.where((sub == owner) & (lane == slot), tile, want)
    want_ref[...] = want


def main_kernel(
    groups, members,
    forcing, viscosity, refinement, pos, plane, hanging, want, solver,
    x_out, r_out,
    S, E, D, ID, W, WK, WJ, F, FT, SEND, RV0, RV1, RZ0, RZ1, GB, G, RQ, RQS, CV, CR, SV,
    send_sem, recv_sem, zsend_sem, zrecv_sem, rq_send, rq_recv, c_send, c_recv, local_sem,
):
    q = lax.axis_index("grp")
    me = lax.axis_index("mem")
    up = lax.rem(q + 1, groups)
    down = lax.rem(q + groups - 1, groups)
    RV = (RV0, RV1)
    RZ = (RZ0, RZ1)

    lane = lax.broadcasted_iota(jnp.int32, (B, LANES), 1)
    sub = lax.broadcasted_iota(jnp.int32, (B, LANES), 0)
    lane16 = lane % EDGE
    group16 = lane // EDGE
    first_k = lane16 == 0
    last_k = lane16 == EDGE - 1
    first_j = lane < EDGE
    last_j = lane >= LANES - EDGE
    odd_1 = lane % 2 == 1
    odd_16 = group16 % 2 == 1

    def roll(v, shift):
        shift = shift % LANES
        return v if shift == 0 else pltpu.roll(v, shift, 1)

    def member(off):
        return lax.rem(me + off, members)

    barrier = pltpu.get_barrier_semaphore()
    for off in range(1, members):
        pl.semaphore_signal(barrier, inc=1, device_id=(q, member(off)), device_id_type=MESH)
    for other in (up, down):
        pl.semaphore_signal(barrier, inc=1, device_id=(other, me), device_id_type=MESH)
    pl.semaphore_wait(barrier, members + 1)

    def request(target, source, slot):
        return pltpu.make_async_remote_copy(
            src_ref=want.at[target], dst_ref=RQ.at[source],
            send_sem=rq_send.at[target], recv_sem=rq_recv.at[slot],
            device_id=(q, target), device_id_type=MESH)

    for off in range(1, members):
        request(member(off), me, me).start()
    RQ[me] = want[me]

    for t in range(3):
        SV[t * 3 * B:(t + 1) * 3 * B, :] = solver[:, t * LANES:(t + 1) * LANES]
    factor_i = jnp.zeros((B, LANES), jnp.int32)
    for b in range(B):
        factor_i = jnp.where(sub == b, refinement[b], factor_i)
    factor = jnp.exp2(-factor_i.astype(F32))
    for v in range(32):
        E[v] = viscosity[:, v * LANES:(v + 1) * LANES] * factor

    def pack_into(planes, row0):
        zero = jnp.zeros((B, LANES), F32)
        p0, p1, p2, p3 = [zero, zero], [zero, zero], [zero, zero], [zero, zero]
        for i in range(EDGE):
            at = lane16 == i
            ih, il = i // 8, i % 8
            tiles = [planes(i, 0), planes(i, 1)]
            for jh in range(2):
                p0[jh] = jnp.where(at, roll(tiles[jh], i), p0[jh])
                p1[jh] = jnp.where(at, roll(tiles[jh], i - 15), p1[jh])
            here = group16 == il
            p2[ih] = jnp.where(here, roll(tiles[0], il * 16), p2[ih])
            p3[ih] = jnp.where(here, roll(tiles[1], il * 16 - 112), p3[ih])
            if i == 0:
                p4 = tiles
            if i == EDGE - 1:
                p5 = tiles
        for d, face in enumerate((p0, p1, p2, p3, p4, p5)):
            for half in range(2):
                F[pl.ds(d * B * ROWS + row0 + half, B, stride=ROWS), :] = face[half]

    def face_copy(par, rows, target, source, slot):
        return pltpu.make_async_remote_copy(
            src_ref=SEND.at[pl.ds(target * CAP, CAP), pl.ds(0, rows), :],
            dst_ref=RV[par].at[pl.ds(source * CAP, CAP), pl.ds(0, rows), :],
            send_sem=send_sem.at[target], recv_sem=recv_sem.at[par, slot],
            device_id=(q, target), device_id_type=MESH)

    def plane_copy(par, rows, which):
        return pltpu.make_async_remote_copy(
            src_ref=FT.at[pl.ds((5 - which) * B, B), pl.ds(0, rows), :],
            dst_ref=RZ[par].at[pl.ds(which * B, B), pl.ds(0, rows), :],
            send_sem=zsend_sem.at[which], recv_sem=zrecv_sem.at[par, which],
            device_id=((up, down)[which], me), device_id_type=MESH)

    def send_faces(par, rows):
        for tile in range(6 * B):
            FT[tile] = F[tile * ROWS:(tile + 1) * ROWS, :]
        for which in range(2):
            plane_copy(par, rows, which).start()

        def fill(m, carry):
            for s in range(CAP):
                tile = RQS[m, 0, s]
                SEND[m * CAP + s] = FT[tile]
            return carry

        lax.fori_loop(0, members, fill, 0)
        for off in range(1, members):
            face_copy(par, rows, member(off), me, me).start()
        for s in range(CAP):
            RV[par][me * CAP + s] = SEND[me * CAP + s]

    def receive_faces(par, rows):
        for off in range(1, members):
            source = member(off)
            face_copy(par, rows, source, source, source).wait_recv()
        for which in range(2):
            plane_copy(par, rows, which).wait_recv()
        for d in range(4):
            for b in range(B):
                GB[pl.ds((d * B + b) * ROWS, ROWS), :] = RV[par][pos[b * 4 + d]]
        for which in range(2):
            for b in range(B):
                tile = which * B + plane[b, which]
                GB[pl.ds(((4 + which) * B + b) * ROWS, ROWS), :] = RZ[par][tile]
        for d in range(6):
            hang = jnp.broadcast_to(hanging[:, d:d + 1], (B, LANES)) == 1
            for row in range(rows):
                g = GB[pl.ds(d * B * ROWS + row, B, stride=ROWS), :]
                pair = g + jnp.where(odd_1, roll(g, 1), roll(g, -1))
                mean = 0.25 * (pair + jnp.where(odd_16, roll(pair, 16), roll(pair, -16)))
                g = jnp.where(hang, mean, g)
                if d == 4:
                    g = jnp.where(q > 0, g, 0.0)
                if d == 5:
                    g = jnp.where(q < groups - 1, g, 0.0)
                G[d * ROWS + row] = g
        for off in range(1, members):
            target = member(off)
            face_copy(par, rows, target, me, me).wait_send()
        for which in range(2):
            plane_copy(par, rows, which).wait_send()

    def k_ghosts(row0, i, jh):
        lower = roll(G[0 * ROWS + row0 + jh], -i)
        upper = roll(G[1 * ROWS + row0 + jh], 15 - i)
        return lower, upper

    def j_ghost(row0, i, jh):
        ih, il = i // 8, i % 8
        if jh == 0:
            return roll(G[2 * ROWS + row0 + ih], -il * 16)
        return roll(G[3 * ROWS + row0 + ih], 112 - il * 16)

    pack_into(lambda i, jh: E[2 * i + jh], 0)
    for off in range(1, members):
        source = member(off)
        request(source, source, source).wait_recv()
    to_smem = pltpu.make_async_copy(RQ, RQS, local_sem)
    to_smem.start()
    to_smem.wait()
    send_faces(0, 2)
    for off in range(1, members):
        request(member(off), me, me).wait_send()
    receive_faces(0, 2)

    for i in range(EDGE):
        e = [E[2 * i], E[2 * i + 1]]
        before = [roll(e[0], 16), roll(e[1], 16)]
        after = [roll(e[0], -16), roll(e[1], -16)]
        for jh in range(2):
            v = 2 * i + jh
            here = e[jh]
            g_low, g_up = k_ghosts(0, i, jh)
            g_j = j_ghost(0, i, jh)
            w0 = 0.5 * (here + jnp.where(first_k, g_low, roll(here, 1)))
            w1 = 0.5 * (here + jnp.where(last_k, g_up, roll(here, -1)))
            if jh == 0:
                w2 = 0.5 * (here + jnp.where(first_j, g_j, before[0]))
                w3 = 0.5 * (here + jnp.where(last_j, after[1], after[0]))
                W[2, v] = jnp.where(first_j, 0.0, w2)
                W[3, v] = w3
                WJ[v] = jnp.where(first_j, w2, 0.0)
            else:
                w2 = 0.5 * (here + jnp.where(first_j, before[0], before[1]))
                w3 = 0.5 * (here + jnp.where(last_j, g_j, after[1]))
                W[2, v] = w2
                W[3, v] = jnp.where(last_j, 0.0, w3)
                WJ[v] = jnp.where(last_j, w3, 0.0)
            low = E[v - 2] if i > 0 else G[4 * ROWS + jh]
            high = E[v + 2] if i < EDGE - 1 else G[5 * ROWS + jh]
            w4 = 0.5 * (here + low)
            w5 = 0.5 * (here + high)
            W[0, v] = jnp.where(first_k, 0.0, w0)
            W[1, v] = jnp.where(last_k, 0.0, w1)
            WK[v] = jnp.where(first_k, w0, jnp.where(last_k, w1, 0.0))
            W[4, v] = w4
            W[5, v] = w5
            diagonal = MASS_TERM * here + w0 + w1 + w2 + w3 + w4 + w5
            D[v] = diagonal
            ID[v] = 1.0 / diagonal

    def cell(v):
        return slice(v * LANES, (v + 1) * LANES)

    def start_smooth(first):
        def body(c, carry):
            def value(i, jh):
                v = 2 * i + jh
                r = forcing[c, :, cell(v)] if first else r_out[c, :, cell(v)]
                s = r * (ID[v] * (1.0 / MIDPOINT))
                S[c, v] = s
                return s
            pack_into(value, c * 2)
            return carry
        lax.fori_loop(0, 3, body, 0)

    def interior(first):
        def body(c, carry):
            for i in range(EDGE):
                s = [S[c, 2 * i], S[c, 2 * i + 1]]
                before = [roll(s[0], 16), roll(s[1], 16)]
                after = [roll(s[0], -16), roll(s[1], -16)]
                for jh in range(2):
                    v = 2 * i + jh
                    here = s[jh]
                    r = forcing[c, :, cell(v)] if first else r_out[c, :, cell(v)]
                    acc = W[0, v] * roll(here, 1) + W[1, v] * roll(here, -1)
                    if jh == 0:
                        acc += W[2, v] * before[0]
                        acc += W[3, v] * jnp.where(last_j, after[1], after[0])
                    else:
                        acc += W[2, v] * jnp.where(first_j, before[0], before[1])
                        acc += W[3, v] * after[1]
                    if i > 0:
                        acc += W[4, v] * S[c, v - 2]
                    if i < EDGE - 1:
                        acc += W[5, v] * S[c, v + 2]
                    r_out[c, :, cell(v)] = r - D[v] * here + acc
                    x_out[c, :, cell(v)] = here if first else x_out[c, :, cell(v)] + here
            return carry
        lax.fori_loop(0, 3, body, 0)

    def finish(follow):
        def body(c, carry):
            row0 = c * 2

            def value(i, jh):
                v = 2 * i + jh
                g_low, g_up = k_ghosts(row0, i, jh)
                r = r_out[c, :, cell(v)]
                r += WK[v] * jnp.where(first_k, g_low, g_up)
                r += WJ[v] * j_ghost(row0, i, jh)
                if i == 0:
                    r += W[4, v] * G[4 * ROWS + row0 + jh]
                if i == EDGE - 1:
                    r += W[5, v] * G[5 * ROWS + row0 + jh]
                r_out[c, :, cell(v)] = r
                if follow is None:
                    return r
                keep, add = follow
                s = r * (ID[v] * add)
                if keep is not None:
                    s += keep * S[c, v]
                S[c, v] = s
                return s

            if follow is None:
                total = jnp.zeros((B, LANES), F32)
                for v in range(32):
                    total += value(v // 2, v % 2)
                CV[c] = total
            else:
                pack_into(value, row0)
            return carry
        lax.fori_loop(0, 3, body, 0)

    def smooth(first, par, at_end):
        rho = 1.0 / SIGMA
        for step in range(DEG):
            send_faces(par, 6)
            interior(first and step == 0)
            receive_faces(par, 6)
            if step < DEG - 1:
                rho_next = 1.0 / (2.0 * SIGMA - rho)
                finish((rho_next * rho, 2.0 * rho_next / HALF_WIDTH))
                rho = rho_next
            else:
                finish(None)
            par = 1 - par

    start_smooth(True)
    smooth(True, 1, None)

    wide = lax.broadcasted_iota(jnp.int32, (B, NC), 1)
    wide_sub = lax.broadcasted_iota(jnp.int32, (B, NC), 0)
    spread = jnp.zeros((B, NC), F32)
    for c in range(3):
        total = jnp.sum(CV[c], axis=1, keepdims=True) * (1.0 / math.sqrt(CELLS))
        spread = jnp.where(wide == me * (3 * B) + 3 * wide_sub + c, total, spread)
    CR[me] = jnp.sum(spread, axis=0, keepdims=True)

    def coarse_copy(target, source, slot):
        return pltpu.make_async_remote_copy(
            src_ref=CR.at[me], dst_ref=CR.at[source],
            send_sem=c_send.at[target], recv_sem=c_recv.at[slot],
            device_id=(q, target), device_id_type=MESH)

    for off in range(1, members):
        coarse_copy(member(off), me, me).start()
    for off in range(1, members):
        source = member(off)
        coarse_copy(source, source, source).wait_recv()
    vector = CR[0]
    for m in range(1, members):
        vector = vector + CR[m]
    for off in range(1, members):
        coarse_copy(member(off), me, me).wait_send()
    vector = jnp.broadcast_to(vector, (B, NC))
    for c in range(3):
        product = jnp.zeros((B, LANES), F32)
        for t in range(3):
            rows = SV[pl.ds(t * 3 * B + c, B, stride=3), :]
            product += rows * vector[:, t * LANES:(t + 1) * LANES]
        correction = jnp.sum(product, axis=1, keepdims=True)
        lifted = jnp.broadcast_to(correction, (B, LANES))
        for v in range(32):
            S[c, v] = lifted
        for d in range(6):
            for half in range(2):
                F[pl.ds(d * B * ROWS + c * 2 + half, B, stride=ROWS), :] = lifted
    send_faces(0, 6)
    interior(False)
    receive_faces(0, 6)
    finish((None, 1.0 / MIDPOINT))
    smooth(False, 1, None)


def local(
    forcing, viscosity, refinement, face_owner, face_block, plane_block, hanging, coarse_solver
):
    groups, members = lax.axis_size("grp"), lax.axis_size("mem")
    vmem = pl.BlockSpec(memory_space=pltpu.VMEM)
    smem = pl.BlockSpec(memory_space=pltpu.SMEM)
    want, pos = pl.pallas_call(
        functools.partial(plan_kernel, members),
        out_shape=(
            jax.ShapeDtypeStruct((members, 1, LANES), jnp.int32),
            jax.ShapeDtypeStruct((4 * B,), jnp.int32),
        ),
        in_specs=[smem, smem],
        out_specs=(vmem, smem),
        scratch_shapes=[pltpu.SMEM((members,), jnp.int32)],
        name="plan",
    )(face_owner, face_block)

    tiles = 2 * EDGE
    dma = pltpu.SemaphoreType.DMA
    field = jax.ShapeDtypeStruct(forcing.shape, F32)
    return pl.pallas_call(
        functools.partial(main_kernel, groups, members),
        out_shape=(field, field),
        in_specs=[vmem, vmem, smem, smem, smem, vmem, vmem, vmem],
        out_specs=(vmem, vmem),
        scratch_shapes=[
            pltpu.VMEM((3, tiles, B, LANES), F32),
            pltpu.VMEM((tiles, B, LANES), F32),
            pltpu.VMEM((tiles, B, LANES), F32),
            pltpu.VMEM((tiles, B, LANES), F32),
            pltpu.VMEM((6, tiles, B, LANES), F32),
            pltpu.VMEM((tiles, B, LANES), F32),
            pltpu.VMEM((tiles, B, LANES), F32),
            pltpu.VMEM((6 * B * ROWS, LANES), F32),
            pltpu.VMEM((6 * B, ROWS, LANES), F32),
            pltpu.VMEM((members * CAP, ROWS, LANES), F32),
            pltpu.VMEM((members * CAP, ROWS, LANES), F32),
            pltpu.VMEM((members * CAP, ROWS, LANES), F32),
            pltpu.VMEM((2 * B, ROWS, LANES), F32),
            pltpu.VMEM((2 * B, ROWS, LANES), F32),
            pltpu.VMEM((6 * B * ROWS, LANES), F32),
            pltpu.VMEM((6 * ROWS, B, LANES), F32),
            pltpu.VMEM((members, 1, LANES), jnp.int32),
            pltpu.SMEM((members, 1, LANES), jnp.int32),
            pltpu.VMEM((3, B, LANES), F32),
            pltpu.VMEM((members, 1, NC), F32),
            pltpu.VMEM((9 * B, LANES), F32),
            dma((members,)),
            dma((2, members)),
            dma((2,)),
            dma((2, 2)),
            dma((members,)),
            dma((members,)),
            dma((members,)),
            dma((members,)),
            dma,
        ],
        compiler_params=pltpu.CompilerParams(collective_id=0, has_side_effects=True),
        name="vcycle",
    )(forcing, viscosity, refinement, pos, plane_block, hanging, want, coarse_solver[0])


def solution(mesh):
    in_specs = (
        P(None, ("grp", "mem"), None),
        P(("grp", "mem"), None),
        P(("grp", "mem")),
        P(("grp", "mem"), None),
        P(("grp", "mem"), None),
        P(("grp", "mem"), None),
        P(("grp", "mem"), None),
        P("grp", "mem", None),
    )
    out_specs = (P(None, ("grp", "mem"), None), P(None, ("grp", "mem"), None))
    return jax.shard_map(local, mesh=mesh, in_specs=in_specs, out_specs=out_specs, check_vma=False)
```
